128 devices in a mesh: stn: 8 (over x_hi, y), tm: 16 (over x_lo, z, core).
Axes of the slice: x: 4 (x_hi: 2, x_lo: 2; x = x_hi * 2 + x_lo), y: 4, z: 4, core: 2. Of those that a mesh axis runs over, the one named last changes fastest.
Arguments:
- voltages: bfloat16 [512, 256, 4096], P('stn', 'tm'), may hold values from -52 to 52
- pfb_taps: float32 [16, 4096], replicated, may hold values from -1.5 to 1.5
- eq_gains: float32 [512, 2048], P('stn'), may hold values from 0.5 to 11
Outputs:
- visibilities: float32 [2048, 512, 512], P(('stn', 'tm'))
The draws below stay inside these ranges and needn't reach their ends.
All inputs are finite; a program needn't handle non-finite values.
Results may differ from the reference program's by a relative error of at most 0.0014.
Values may be sent and summed in bfloat16 or wider, within the bound.
No kernel may reach another device: no remote copies, remote signals or barrier semaphores. Data moves between devices by JAX's collectives and lax.ppermute only.
A program may use at most 448 MiB of HBM per device.

```python
import math
import jax
import jax.numpy as jnp
from jax import lax

CHANNELS = 2048
TAPS = 16
INPUTS = 512
FRAMES = 256
FFT_LEN = 4096


def draw_voltages(key, part):
    keys = jax.random.split(key, 4)
    shape = (INPUTS, FRAMES, FFT_LEN)
    position = jnp.arange(FRAMES, dtype=jnp.float32) / (FRAMES - 1)
    coupling = jax.random.uniform(keys[2], (INPUTS, 1, 1), jnp.float32, 0.2, 1.0)
    roughness = jnp.exp(jax.random.uniform(keys[3], (INPUTS, FRAMES, 1), jnp.float32, math.log(0.5), math.log(2.0)))
    noise = jnp.clip(jax.random.normal(keys[0], shape, jnp.float32), -4.0, 4.0)
    common = jnp.clip(jax.random.normal(keys[1], (1, FRAMES, FFT_LEN), jnp.float32), -4.0, 4.0)
    drift = jnp.exp(0.5 * math.log(10.0) * position)
    return ((noise + coupling * common) * roughness * drift[None, :, None]).astype(jnp.bfloat16)


def draw_eq_gains(key, part):
    channel_pos = jnp.arange(CHANNELS, dtype=jnp.float32) / (CHANNELS - 1)
    rough_gain = jnp.exp(jax.random.uniform(key, (INPUTS, CHANNELS), jnp.float32, math.log(0.5), math.log(2.0)))
    bandpass = jnp.exp(0.5 * math.log(10.0) * channel_pos)
    return rough_gain * bandpass[None, :]


def bell_draw(stream_key, dims, spread, bound, kind=jnp.bfloat16):
    array = spread * jax.random.normal(stream_key, dims, jnp.float32)
    return jnp.clip(array, min=-bound, max=bound).astype(kind)


def setup_inputs(seed: int = 0) -> dict:
    arg_keys = jax.random.split(jax.random.key(seed), 4)
    voltages = draw_voltages(jax.random.fold_in(arg_keys[3], 71), 0)
    pfb_taps = bell_draw(arg_keys[1], (TAPS, FFT_LEN), TAPS ** -0.5, 1.5, jnp.float32)
    eq_gains = draw_eq_gains(jax.random.fold_in(arg_keys[3], 71), 0)
    return {"voltages": voltages, "pfb_taps": pfb_taps, "eq_gains": eq_gains}


chan_block = 8

def channelize(volt_row, gain_row, pfb_taps):
    frames = volt_row.astype(jnp.float32)
    history_len = TAPS - 1
    padded = jnp.concatenate([jnp.zeros((history_len, FFT_LEN), jnp.float32), frames], axis=0)
    filtered = jnp.zeros((FRAMES, FFT_LEN), jnp.float32)
    for tap_index in range(TAPS):
        first_row = history_len - tap_index
        filtered = filtered + pfb_taps[tap_index][None, :] * padded[first_row:first_row + FRAMES]
    spectrum = jnp.fft.rfft(filtered, axis=-1)[:, :CHANNELS]
    spec_re = (jnp.real(spectrum) * gain_row[None, :]).astype(jnp.bfloat16)
    spec_im = (jnp.imag(spectrum) * gain_row[None, :]).astype(jnp.bfloat16)
    return (spec_re, spec_im)

def reference(voltages, pfb_taps, eq_gains):
    spec_re, spec_im = lax.map(lambda pair: channelize(pair[0], pair[1], pfb_taps), (voltages, eq_gains))
    power = lax.optimization_barrier(jnp.sum(jnp.square(spec_re.astype(jnp.float32)) + jnp.square(spec_im.astype(jnp.float32)), axis=(1, 2)))
    scale = lax.rsqrt(power / (FRAMES * CHANNELS) + 1e-06)
    weight = scale[:, None] * scale[None, :] / FRAMES
    row_ids = lax.broadcasted_iota(jnp.int32, (INPUTS, INPUTS), 0)
    col_ids = lax.broadcasted_iota(jnp.int32, (INPUTS, INPUTS), 1)
    lower = row_ids >= col_ids
    re_blocks = jnp.transpose(spec_re, (2, 0, 1)).reshape(CHANNELS // chan_block, chan_block, INPUTS, FRAMES)
    im_blocks = jnp.transpose(spec_im, (2, 0, 1)).reshape(CHANNELS // chan_block, chan_block, INPUTS, FRAMES)
    highest = lax.Precision.HIGHEST

    def correlate(pair):
        part_re = pair[0].astype(jnp.float32)
        part_im = pair[1].astype(jnp.float32)
        vis_re = jnp.einsum('cat,cbt->cab', part_re, part_re, precision=highest) + jnp.einsum('cat,cbt->cab', part_im, part_im, precision=highest)
        vis_im = jnp.einsum('cat,cbt->cab', part_im, part_re, precision=highest) - jnp.einsum('cat,cbt->cab', part_re, part_im, precision=highest)
        return jnp.where(lower[None], vis_re, vis_im) * weight[None]
    packed = lax.map(correlate, (re_blocks, im_blocks))
    return packed.reshape(CHANNELS, INPUTS, INPUTS)
```

```python
import functools
import math

import jax
import jax.numpy as jnp
import numpy as np
from jax import lax
from jax.experimental import pallas as pl
from jax.experimental.pallas import tpu as pltpu
from jax.sharding import PartitionSpec as P

LANES = 128
RADIX = 32
SLOTS = 16
TAPS = 16
HALO = 8
PITCH = 32
GROUP = 8
Q_CHUNKS = (4, 4, 4, 4)
POWER_CHUNK = 1
INPUT_CHUNKS = 4


def real_dft(values):
    count = len(values)
    if count == 1:
        return [(values[0], None)]
    if count == 2:
        return [(values[0] + values[1], None), (values[0] - values[1], None)]
    even = real_dft(values[0::2])
    odd = real_dft(values[1::2])
    half, quarter = count // 2, count // 4
    bins = [None] * (half + 1)
    bins[0] = (even[0][0] + odd[0][0], None)
    bins[half] = (even[0][0] - odd[0][0], None)
    bins[quarter] = (even[quarter][0], -odd[quarter][0])
    for k in range(1, quarter):
        c, s = math.cos(2 * math.pi * k / count), math.sin(2 * math.pi * k / count)
        re, im = odd[k]
        if 8 * k == count:
            turned_re, turned_im = (re + im) * c, (im - re) * c
        else:
            turned_re, turned_im = re * c + im * s, im * c - re * s
        bins[k] = (even[k][0] + turned_re, even[k][1] + turned_im)
        bins[half - k] = (even[k][0] - turned_re, turned_im - even[k][1])
    return bins


def filter_body(flag_ref, own_ref, before_ref, after_ref, taps_ref, *rest):
    out_ref, frames_ref, filtered_ref = rest[-3:]
    tiles = own_ref.shape[2] // LANES
    frames = own_ref.shape[1]
    span = GROUP * PITCH
    flag = flag_ref[0]

    def widen(tile, carry):
        lanes = pl.ds(pl.multiple_of(tile * LANES, LANES), LANES)
        own = own_ref[:, :, lanes].astype(jnp.float32)
        before = before_ref[:, :, lanes].astype(jnp.float32)
        after = after_ref[:, :, lanes].astype(jnp.float32)
        for i in range(GROUP):
            row = pl.multiple_of(tile * span + i * PITCH, 8)
            frames_ref[pl.ds(row, HALO), :] = before[i]
            frames_ref[pl.ds(row + HALO, frames), :] = own[i]
            frames_ref[pl.ds(row + HALO + frames, HALO), :] = after[i]
        return carry

    lax.fori_loop(0, tiles, widen, 0)

    def fir(tile, carry):
        lanes = pl.ds(pl.multiple_of(tile * LANES, LANES), LANES)
        taps = [
            jnp.broadcast_to(taps_ref[p : p + 1, lanes], (GROUP, LANES)) for p in range(TAPS)
        ]
        for half in range(2):
            sums = [None] * HALO
            for r in range(1 + 8 * half, 24 + 8 * half):
                frame = frames_ref[pl.ds(tile * span + r, GROUP, stride=PITCH), :]
                if half == 1 and r < HALO + frames:
                    frame = frame * flag
                for j in range(HALO):
                    p = j + 8 * half + TAPS - r
                    if 0 <= p < TAPS:
                        term = taps[p] * frame
                        sums[j] = term if sums[j] is None else sums[j] + term
            for j in range(HALO):
                filtered_ref[j + 8 * half, tile] = sums[j]
        return carry

    lax.fori_loop(0, tiles, fir, 0)

    def butterfly(frame, carry):
        bins = real_dft([filtered_ref[frame, tile] for tile in range(tiles)])
        out_ref[0, frame, :, :LANES] = bins[0][0]
        out_ref[0, frame, :, LANES:] = bins[RADIX // 2][0]
        for q in range(1, SLOTS):
            out_ref[q, frame, :, :LANES] = bins[q][0]
            out_ref[q, frame, :, LANES:] = bins[q][1]
        return carry

    lax.fori_loop(0, frames, butterfly, 0)


def filter_call(flag, voltages, before, after, taps, partial, chunk):
    inputs, frames, length = voltages.shape
    groups = before.shape[0] // GROUP
    base = chunk * groups
    tiles = length // LANES
    operands = [flag, voltages, before, after, taps]
    in_specs = [
        pl.BlockSpec(memory_space=pltpu.SMEM),
        pl.BlockSpec((GROUP, frames, length), lambda g: (g + base, 0, 0)),
        pl.BlockSpec((GROUP, HALO, length), lambda g: (g, 0, 0)),
        pl.BlockSpec((GROUP, HALO, length), lambda g: (g, 0, 0)),
        pl.BlockSpec((TAPS, length), lambda g: (0, 0)),
    ]
    aliases = {}
    if partial is not None:
        operands.append(partial)
        in_specs.append(pl.BlockSpec(memory_space=pl.ANY))
        aliases = {5: 0}
    return pl.pallas_call(
        filter_body,
        name="filter",
        grid=(groups,),
        in_specs=in_specs,
        out_specs=pl.BlockSpec((SLOTS, frames, GROUP, 2 * LANES), lambda g: (0, 0, g + base, 0)),
        out_shape=jax.ShapeDtypeStruct((SLOTS, frames, inputs, 2 * LANES), jnp.float32),
        scratch_shapes=[
            pltpu.VMEM((tiles * GROUP * PITCH, LANES), jnp.float32),
            pltpu.VMEM((frames, tiles, GROUP, LANES), jnp.float32),
        ],
        input_output_aliases=aliases,
        compiler_params=pltpu.CompilerParams(vmem_limit_bytes=48 * 2**20),
    )(*operands)


def matmul_nt(left, right):
    return lax.dot_general(
        left, right, (((1,), (1,)), ((), ())), preferred_element_type=jnp.float32
    )


def split(value):
    high = value.astype(jnp.bfloat16)
    return high, (value - high.astype(jnp.float32)).astype(jnp.bfloat16)


def spectrum_body(
    first, part_ref, cos_ref, sin_ref, twist_cos_ref, twist_sin_ref, gain_ref, out_ref, power_ref, turn_ref
):
    step = pl.program_id(0)
    is_first = (step + first) == 0
    rows = part_ref.shape[1] * part_ref.shape[2]
    odd = lax.broadcasted_iota(jnp.int32, (LANES, LANES), 0) % 2 == 1
    twist_cos = jnp.where(odd, twist_cos_ref[0, 1:2, :], twist_cos_ref[0, 0:1, :])
    twist_sin = jnp.where(odd, twist_sin_ref[0, 1:2, :], twist_sin_ref[0, 0:1, :])
    cos = cos_ref[...] * twist_cos - sin_ref[...] * twist_sin
    sin = sin_ref[...] * twist_cos + cos_ref[...] * twist_sin
    special = jnp.where(is_first, 1.0, 0.0)
    drop = jnp.where(odd, special, 0.0)
    keep = 1.0 - drop
    sign = jnp.where(odd, -1.0, 1.0) * (1.0 - special)
    matrix = jnp.concatenate(
        [
            jnp.concatenate([cos * keep, sign * sin + drop * cos], axis=1),
            jnp.concatenate([-sin * keep, sign * cos - drop * sin], axis=1),
        ],
        axis=0,
    )
    matrix_high, matrix_low = split(matrix)
    part = part_ref[0].reshape(rows, 2 * LANES)
    gain = gain_ref[0]
    width = 2 * LANES
    for block in range(rows // width):
        part_high, part_low = split(part[block * width : (block + 1) * width])
        spec = (
            matmul_nt(matrix_high, part_high)
            + matmul_nt(matrix_high, part_low)
            + matmul_nt(matrix_low, part_high)
        )
        for side in range(2):
            for tile in range(width // LANES):
                value = spec[side * LANES : (side + 1) * LANES, tile * LANES : (tile + 1) * LANES]
                turn_ref[side, pl.ds(block * (width // LANES) + tile, LANES, stride=8), :] = (
                    value * gain
                )
    power = jnp.zeros((8, LANES), jnp.float32)
    for side in range(2):
        rounded = turn_ref[side].reshape(LANES, 8, LANES).astype(jnp.bfloat16)
        out_ref[:, side] = rounded
        wide = rounded.astype(jnp.float32)
        power = power + jnp.sum(wide * wide, axis=0)

    @pl.when(step == 0)
    def _():
        power_ref[...] = power

    @pl.when(step > 0)
    def _():
        power_ref[...] += power


def spectrum_call(partial, tables, gains, first, count, spare):
    _, frames, inputs, width = partial.shape
    cos, sin, twist_cos, twist_sin = tables
    whole = lambda q: (0, 0)
    pick = lambda q: (q + first, 0, 0)
    return pl.pallas_call(
        functools.partial(spectrum_body, first),
        name="spectrum",
        grid=(count,),
        in_specs=[
            pl.BlockSpec((1, frames, inputs, width), lambda q: (q + first, 0, 0, 0)),
            pl.BlockSpec((LANES, LANES), whole),
            pl.BlockSpec((LANES, LANES), whole),
            pl.BlockSpec((1, 2, LANES), pick),
            pl.BlockSpec((1, 2, LANES), pick),
            pl.BlockSpec((1, LANES, LANES), pick),
        ],
        out_specs=[
            pl.BlockSpec((LANES, 2, 8, LANES), lambda q: (0, q, 0, 0)),
            pl.BlockSpec((8, LANES), whole),
        ],
        out_shape=[
            jax.ShapeDtypeStruct((LANES, 2 * count + spare, 8, LANES), jnp.bfloat16),
            jax.ShapeDtypeStruct((8, LANES), jnp.float32),
        ],
        scratch_shapes=[pltpu.VMEM((2, 8 * LANES, LANES), jnp.float32)],
        compiler_params=pltpu.CompilerParams(vmem_limit_bytes=48 * 2**20),
    )(partial, cos, sin, twist_cos, twist_sin, gains)


def stamp_body(*refs):
    out_ref = refs[-1]
    total = refs[0][...]
    for ref in refs[1:-2]:
        total = total + ref[...]
    total = jnp.sum(total, axis=0, keepdims=True)
    high, rest = total.astype(jnp.bfloat16), total
    rest = rest - high.astype(jnp.float32)
    middle = rest.astype(jnp.bfloat16)
    low = (rest - middle.astype(jnp.float32)).astype(jnp.bfloat16)
    row = lax.broadcasted_iota(jnp.int32, (8, LANES), 0)
    tile = jnp.where(row == 0, high.astype(jnp.float32), 0.0)
    tile = jnp.where(row == 1, middle.astype(jnp.float32), tile)
    tile = jnp.where(row == 2, low.astype(jnp.float32), tile).astype(jnp.bfloat16)
    out_ref[...] = jnp.broadcast_to(tile[None, None], out_ref.shape)


def stamp_call(powers, payload):
    last = payload.shape[1] - 1
    return pl.pallas_call(
        stamp_body,
        name="stamp",
        grid=(1,),
        in_specs=[pl.BlockSpec((8, LANES), lambda i: (0, 0))] * len(powers)
        + [pl.BlockSpec(memory_space=pl.ANY)],
        out_specs=pl.BlockSpec((LANES, 1, 8, LANES), lambda i: (0, last, 0, 0)),
        out_shape=jax.ShapeDtypeStruct(payload.shape, payload.dtype),
        input_output_aliases={len(powers): 0},
    )(*powers, payload)


def correlate_body(groups, odd_ref, spec_ref, row_ref, col_ref, *rest):
    out_ref, left_ref, swapped_ref = rest[-3:]
    blocks = spec_ref.shape[0] // groups
    half = LANES // 2
    depth = blocks * 8
    for side in range(2):
        for s in range(groups):
            tile = spec_ref[s * blocks : (s + 1) * blocks, side].reshape(depth, LANES).T
            rows = slice(s * half, (s + 1) * half)
            for part in range(2):
                piece = tile[part * half : (part + 1) * half]
                at = part * depth
                left_ref[rows, side * 2 * depth + at : side * 2 * depth + at + depth] = piece
                other = (1 - side) * 2 * depth + at
                swapped_ref[rows, other : other + depth] = -piece if side == 0 else piece
    total = groups * half
    mid = total // 2
    for bi in range(2):
        for bj in range(2):
            rows, cols = slice(bi * mid, (bi + 1) * mid), slice(bj * mid, (bj + 1) * mid)
            weight = col_ref[rows, :] * row_ref[:, cols]
            right = left_ref[cols, :]
            if bi >= bj:
                real = matmul_nt(left_ref[rows, :], right)
            if bi <= bj:
                imag = matmul_nt(swapped_ref[rows, :], right)
            if bi == bj:
                lower = lax.broadcasted_iota(jnp.int32, (mid, mid), 0) >= lax.broadcasted_iota(
                    jnp.int32, (mid, mid), 1
                )
                value = jnp.where(lower, real, imag)
            else:
                value = real if bi > bj else imag
            out_ref[0, rows, cols] = value * weight


def correlate_call(odd, spectra, scale_row, scale_col, visibilities, first, count, groups, channels):
    total = scale_row.shape[1]
    place = lambda q, odd: (jnp.where(odd[0] == 1, (SLOTS - first - q) % SLOTS, first + q), 0, 0)
    operands = [odd, spectra, scale_row, scale_col]
    in_specs = [
        pl.BlockSpec((spectra.shape[0], 2, 8, LANES), lambda q, odd: (0, q, 0, 0)),
        pl.BlockSpec((1, total), lambda q, odd: (0, 0)),
        pl.BlockSpec((total, 1), lambda q, odd: (0, 0)),
    ]
    aliases = {}
    if visibilities is not None:
        operands.append(visibilities)
        in_specs.append(pl.BlockSpec(memory_space=pl.ANY))
        aliases = {4: 0}
    depth = 2 * spectra.shape[0] // groups * 16
    return pl.pallas_call(
        functools.partial(correlate_body, groups),
        name="correlate",
        grid_spec=pltpu.PrefetchScalarGridSpec(
            num_scalar_prefetch=1,
            grid=(count,),
            in_specs=in_specs,
            out_specs=pl.BlockSpec((1, total, total), place),
            scratch_shapes=[
                pltpu.VMEM((total, depth), jnp.bfloat16),
                pltpu.VMEM((total, depth), jnp.bfloat16),
            ],
        ),
        out_shape=jax.ShapeDtypeStruct((channels, total, total), jnp.float32),
        input_output_aliases=aliases,
        compiler_params=pltpu.CompilerParams(vmem_limit_bytes=48 * 2**20),
    )(*operands)


def trig_tables():
    dest = np.arange(LANES)[:, None]
    sample = np.arange(LANES)[None, :]
    angle = 2 * np.pi / 256 * ((dest * sample) % 256)
    offset = np.stack([np.arange(SLOTS), (SLOTS - np.arange(SLOTS)) % SLOTS], axis=1)
    twist = 2 * np.pi / 4096 * (offset[:, :, None] * np.arange(LANES)[None, None, :])
    tables = (np.cos(angle), np.sin(angle), np.cos(twist), np.sin(twist))
    return [jnp.asarray(table, jnp.float32) for table in tables]


def arrange_gains(gains):
    inputs, channels = gains.shape
    turned = gains.T.reshape(channels // (2 * SLOTS), 2, SLOTS, inputs)
    straight = turned[:, 0]
    reversed_ = jnp.roll(jnp.flip(turned[:, 1], axis=1), 1, axis=1)
    both = jnp.stack([straight, reversed_], axis=1).reshape(channels // SLOTS, SLOTS, inputs)
    by_slot = jnp.transpose(both, (1, 0, 2))
    return jnp.concatenate([by_slot, by_slot], axis=2)


def per_device(voltages, pfb_taps, eq_gains):
    inputs, frames, length = voltages.shape
    stations, times = lax.axis_size("stn"), lax.axis_size("tm")
    channels = eq_gains.shape[1]
    here = lax.axis_index("tm")
    forward = [(i, i + 1) for i in range(times - 1)]
    backward = [((i + 1) % times, i) for i in range(times)]
    flag = jnp.where(here == times - 1, 0.0, 1.0).astype(jnp.float32).reshape(1)
    size = inputs // INPUT_CHUNKS
    halos = []
    for chunk in range(INPUT_CHUNKS):
        block = voltages[chunk * size : (chunk + 1) * size]
        halos.append(
            (
                lax.ppermute(block[:, frames - HALO :], "tm", forward),
                lax.ppermute(block[:, :HALO], "tm", backward),
            )
        )
    gains = arrange_gains(eq_gains)
    tables = trig_tables()
    partial = None
    for chunk in range(INPUT_CHUNKS):
        before, after = halos[chunk]
        partial = filter_call(flag, voltages, before, after, pfb_taps, partial, chunk)
    payloads, powers, first = [], [], 0
    for index, count in enumerate(Q_CHUNKS):
        spare = 1 if index == POWER_CHUNK else 0
        payload, power = spectrum_call(partial, tables, gains, first, count, spare)
        payloads.append(payload)
        powers.append(power)
        first += count
    payloads[POWER_CHUNK] = stamp_call(powers, payloads[POWER_CHUNK])
    received = [
        lax.all_to_all(payload, ("stn", "tm"), split_axis=0, concat_axis=0, tiled=True)
        for payload in payloads
    ]
    parts = received[POWER_CHUNK][:, 2 * Q_CHUNKS[POWER_CHUNK], :3].astype(jnp.float32)
    parts = parts.reshape(stations, times, 3, LANES // inputs, inputs)
    power = jnp.sum(parts, axis=(1, 2, 3)).reshape(stations * inputs)
    all_frames = frames * times
    scale = lax.rsqrt(power / (all_frames * channels) + 1e-06)
    scale_row = (scale / all_frames).reshape(1, -1)
    scale_col = scale.reshape(-1, 1)
    odd = (here % 2).astype(jnp.int32).reshape(1)
    visibilities, first = None, 0
    for index, count in enumerate(Q_CHUNKS):
        visibilities = correlate_call(
            odd,
            received[index],
            scale_row,
            scale_col,
            visibilities,
            first,
            count,
            stations,
            channels // (stations * times),
        )
        first += count
    return visibilities


def solution(mesh):
    in_specs = (P("stn", "tm", None), P(), P("stn", None))
    out_specs = P(("stn", "tm"), None, None)
    return jax.shard_map(
        per_device, mesh=mesh, in_specs=in_specs, out_specs=out_specs, check_vma=False
    )
```

```python
import functools
import math

import jax
import jax.numpy as jnp
import numpy as np
from jax import lax
from jax.experimental import pallas as pl
from jax.experimental.pallas import tpu as pltpu
from jax.sharding import PartitionSpec as P

LANES = 128
RADIX = 32
SLOTS = 16
TAPS = 16
HALO = 8
PITCH = 40
GROUP = 8
Q_CHUNKS = (4, 8, 4)
POWER_CHUNK = 1
IN_FLIGHT = 3
SPECTRUM_BLOCK = 4
CORRELATE_BLOCK = 1
INPUT_CHUNKS = (16, 16, 16, 16)


def real_dft(values):
    count = len(values)
    if count == 1:
        return [(values[0], None)]
    if count == 2:
        return [(values[0] + values[1], None), (values[0] - values[1], None)]
    even = real_dft(values[0::2])
    odd = real_dft(values[1::2])
    half, quarter = count // 2, count // 4
    bins = [None] * (half + 1)
    bins[0] = (even[0][0] + odd[0][0], None)
    bins[half] = (even[0][0] - odd[0][0], None)
    bins[quarter] = (even[quarter][0], -odd[quarter][0])
    for k in range(1, quarter):
        c, s = math.cos(2 * math.pi * k / count), math.sin(2 * math.pi * k / count)
        re, im = odd[k]
        if 8 * k == count:
            turned_re, turned_im = (re + im) * c, (im - re) * c
        else:
            turned_re, turned_im = re * c + im * s, im * c - re * s
        bins[k] = (even[k][0] + turned_re, even[k][1] + turned_im)
        bins[half - k] = (even[k][0] - turned_re, turned_im - even[k][1])
    return bins


def filter_body(flag_ref, own_ref, before_ref, after_ref, taps_ref, *rest):
    out_ref, frames_ref, filtered_ref = rest[-3:]
    tiles = own_ref.shape[2] // LANES
    frames = own_ref.shape[1]
    span = GROUP * PITCH
    flag = flag_ref[0]

    def widen(tile, carry):
        lanes = pl.ds(pl.multiple_of(tile * LANES, LANES), LANES)
        own = own_ref[:, :, lanes].astype(jnp.float32)
        before = before_ref[:, :, lanes].astype(jnp.float32)
        after = after_ref[:, :, lanes].astype(jnp.float32)
        for i in range(GROUP):
            row = pl.multiple_of(tile * span + i * PITCH, 8)
            frames_ref[pl.ds(row, HALO), :] = before[i]
            frames_ref[pl.ds(row + HALO, frames), :] = own[i]
            frames_ref[pl.ds(row + HALO + frames, HALO), :] = after[i]
        return carry

    lax.fori_loop(0, tiles, widen, 0)

    def fir(tile, carry):
        lanes = pl.ds(pl.multiple_of(tile * LANES, LANES), LANES)
        taps = [
            jnp.broadcast_to(taps_ref[p : p + 1, lanes], (GROUP, LANES)) for p in range(TAPS)
        ]
        for half in range(2):
            sums = [None] * HALO
            for r in range(1 + 8 * half, 24 + 8 * half):
                frame = frames_ref[pl.ds(tile * span + r, GROUP, stride=PITCH), :]
                if half == 1 and r < HALO + frames:
                    frame = frame * flag
                for j in range(HALO):
                    p = j + 8 * half + TAPS - r
                    if 0 <= p < TAPS:
                        term = taps[p] * frame
                        sums[j] = term if sums[j] is None else sums[j] + term
            for j in range(HALO):
                filtered_ref[j + 8 * half, tile] = sums[j]
        return carry

    lax.fori_loop(0, tiles, fir, 0)

    def butterfly(frame, carry):
        bins = real_dft([filtered_ref[frame, tile] for tile in range(tiles)])
        out_ref[0, frame, :, :LANES] = bins[0][0]
        out_ref[0, frame, :, LANES:] = bins[RADIX // 2][0]
        for q in range(1, SLOTS):
            out_ref[q, frame, :, :LANES] = bins[q][0]
            out_ref[q, frame, :, LANES:] = bins[q][1]
        return carry

    lax.fori_loop(0, frames, butterfly, 0)


def filter_call(flag, voltages, before, after, taps, partial, start):
    inputs, frames, length = voltages.shape
    groups = before.shape[0] // GROUP
    base = start // GROUP
    tiles = length // LANES
    operands = [flag, voltages, before, after, taps]
    in_specs = [
        pl.BlockSpec(memory_space=pltpu.SMEM),
        pl.BlockSpec((GROUP, frames, length), lambda g: (g + base, 0, 0)),
        pl.BlockSpec((GROUP, HALO, length), lambda g: (g, 0, 0)),
        pl.BlockSpec((GROUP, HALO, length), lambda g: (g, 0, 0)),
        pl.BlockSpec((TAPS, length), lambda g: (0, 0)),
    ]
    aliases = {}
    if partial is not None:
        operands.append(partial)
        in_specs.append(pl.BlockSpec(memory_space=pl.ANY))
        aliases = {5: 0}
    return pl.pallas_call(
        filter_body,
        name="filter",
        cost_estimate=pl.CostEstimate(
            flops=groups * 5 * 10**9, transcendentals=0, bytes_accessed=groups * 4 * 2**20
        ),
        grid=(groups,),
        in_specs=in_specs,
        out_specs=pl.BlockSpec((SLOTS, frames, GROUP, 2 * LANES), lambda g: (0, 0, g + base, 0)),
        out_shape=jax.ShapeDtypeStruct((SLOTS, frames, inputs, 2 * LANES), jnp.float32),
        scratch_shapes=[
            pltpu.VMEM((tiles * GROUP * PITCH, LANES), jnp.float32),
            pltpu.VMEM((frames, tiles, GROUP, LANES), jnp.float32),
        ],
        input_output_aliases=aliases,
        compiler_params=pltpu.CompilerParams(vmem_limit_bytes=56 * 2**20),
    )(*operands)


def matmul_nt(left, right):
    return lax.dot_general(
        left, right, (((1,), (1,)), ((), ())), preferred_element_type=jnp.float32
    )


def split(value):
    high = value.astype(jnp.bfloat16)
    return high, (value - high.astype(jnp.float32)).astype(jnp.bfloat16)


def spectrum_body(
    first, part_ref, cos_ref, sin_ref, twist_cos_ref, twist_sin_ref, gain_ref, out_ref, power_ref, turn_ref
):
    step = pl.program_id(0)
    slots, frames, inputs, width = part_ref.shape
    rows = frames * inputs
    odd = lax.broadcasted_iota(jnp.int32, (LANES, LANES), 0) % 2 == 1
    flip = jnp.where(odd, -1.0, 1.0)
    per_block = width // LANES
    total = None
    for slot in range(slots):
        twist_cos = jnp.where(odd, twist_cos_ref[slot, 1:2, :], twist_cos_ref[slot, 0:1, :])
        twist_sin = jnp.where(odd, twist_sin_ref[slot, 1:2, :], twist_sin_ref[slot, 0:1, :])
        cos = cos_ref[...] * twist_cos - sin_ref[...] * twist_sin
        sin = sin_ref[...] * twist_cos + cos_ref[...] * twist_sin
        parts = [cos, flip * sin, -sin, flip * cos]
        if first == 0 and slot == 0:
            special = jnp.where(step == 0, 1.0, 0.0)
            drop = jnp.where(odd, special, 0.0)
            keep = 1.0 - drop
            sign = flip * (1.0 - special)
            parts = [cos * keep, sign * sin + drop * cos, -sin * keep, sign * cos - drop * sin]
        matrix = jnp.concatenate(
            [jnp.concatenate(parts[:2], axis=1), jnp.concatenate(parts[2:], axis=1)], axis=0
        )
        matrix_high, matrix_low = split(matrix)
        part = part_ref[slot].reshape(rows, width)
        gain = gain_ref[slot]
        for block in range(rows // width):
            part_high, part_low = split(part[block * width : (block + 1) * width])
            spec = (
                matmul_nt(matrix_high, part_high)
                + matmul_nt(matrix_high, part_low)
                + matmul_nt(matrix_low, part_high)
            )
            for side in range(2):
                for tile in range(per_block):
                    value = spec[
                        side * LANES : (side + 1) * LANES, tile * LANES : (tile + 1) * LANES
                    ]
                    turn_ref[slot % 2, side, pl.ds(block * per_block + tile, LANES, stride=8), :] = (
                        value * gain
                    )
        for side in range(2):
            rounded = turn_ref[slot % 2, side].reshape(LANES, 8, LANES).astype(jnp.bfloat16)
            out_ref[:, 2 * slot + side] = rounded
            wide = rounded.astype(jnp.float32)
            power = jnp.sum(wide * wide, axis=0)
            total = power if total is None else total + power

    @pl.when(step == 0)
    def _():
        power_ref[...] = total

    @pl.when(step > 0)
    def _():
        power_ref[...] += total


def spectrum_call(partial, tables, gains, first, count, spare):
    _, frames, inputs, width = partial.shape
    cos, sin, twist_cos, twist_sin = tables
    whole = lambda q: (0, 0)
    block = SPECTRUM_BLOCK
    start = first // block
    pick = lambda q: (q + start, 0, 0)
    return pl.pallas_call(
        functools.partial(spectrum_body, first),
        name="spectrum",
        grid=(count // block,),
        in_specs=[
            pl.BlockSpec((block, frames, inputs, width), lambda q: (q + start, 0, 0, 0)),
            pl.BlockSpec((LANES, LANES), whole),
            pl.BlockSpec((LANES, LANES), whole),
            pl.BlockSpec((block, 2, LANES), pick),
            pl.BlockSpec((block, 2, LANES), pick),
            pl.BlockSpec((block, LANES, LANES), pick),
        ],
        out_specs=[
            pl.BlockSpec((LANES, 2 * block, 8, LANES), lambda q: (0, q, 0, 0)),
            pl.BlockSpec((8, LANES), whole),
        ],
        out_shape=[
            jax.ShapeDtypeStruct((LANES, 2 * count + spare, 8, LANES), jnp.bfloat16),
            jax.ShapeDtypeStruct((8, LANES), jnp.float32),
        ],
        scratch_shapes=[pltpu.VMEM((2, 2, 8 * LANES, LANES), jnp.float32)],
        compiler_params=pltpu.CompilerParams(vmem_limit_bytes=56 * 2**20),
    )(partial, cos, sin, twist_cos, twist_sin, gains)


def stamp_body(*refs):
    out_ref = refs[-1]
    total = refs[0][...]
    for ref in refs[1:-2]:
        total = total + ref[...]
    total = jnp.sum(total, axis=0, keepdims=True)
    high, rest = total.astype(jnp.bfloat16), total
    rest = rest - high.astype(jnp.float32)
    middle = rest.astype(jnp.bfloat16)
    low = (rest - middle.astype(jnp.float32)).astype(jnp.bfloat16)
    row = lax.broadcasted_iota(jnp.int32, (8, LANES), 0)
    tile = jnp.where(row == 0, high.astype(jnp.float32), 0.0)
    tile = jnp.where(row == 1, middle.astype(jnp.float32), tile)
    tile = jnp.where(row == 2, low.astype(jnp.float32), tile).astype(jnp.bfloat16)
    out_ref[...] = jnp.broadcast_to(tile[None, None], out_ref.shape)


def stamp_call(powers, payload):
    last = payload.shape[1] - 1
    return pl.pallas_call(
        stamp_body,
        name="stamp",
        grid=(1,),
        in_specs=[pl.BlockSpec((8, LANES), lambda i: (0, 0))] * len(powers)
        + [pl.BlockSpec(memory_space=pl.ANY)],
        out_specs=pl.BlockSpec((LANES, 1, 8, LANES), lambda i: (0, last, 0, 0)),
        out_shape=jax.ShapeDtypeStruct(payload.shape, payload.dtype),
        input_output_aliases={len(powers): 0},
    )(*powers, payload)


def correlate_body(groups, odd_ref, spec_ref, row_ref, col_ref, *rest):
    out_ref, left_ref, swapped_ref = rest[-3:]
    slot = pl.program_id(1)
    blocks = spec_ref.shape[0] // groups
    half = LANES // 2
    depth = blocks * 8
    for side in range(2):
        for s in range(groups):
            tile = spec_ref[s * blocks : (s + 1) * blocks, 2 * slot + side].reshape(depth, LANES).T
            rows = slice(s * half, (s + 1) * half)
            for part in range(2):
                piece = tile[part * half : (part + 1) * half]
                at = part * depth
                left_ref[rows, side * 2 * depth + at : side * 2 * depth + at + depth] = piece
                other = (1 - side) * 2 * depth + at
                swapped_ref[rows, other : other + depth] = -piece if side == 0 else piece
    total = groups * half
    mid = total // 2
    for bi in range(2):
        for bj in range(2):
            rows, cols = slice(bi * mid, (bi + 1) * mid), slice(bj * mid, (bj + 1) * mid)
            weight = col_ref[rows, :] * row_ref[:, cols]
            right = left_ref[cols, :]
            if bi >= bj:
                real = matmul_nt(left_ref[rows, :], right)
            if bi <= bj:
                imag = matmul_nt(swapped_ref[rows, :], right)
            if bi == bj:
                lower = lax.broadcasted_iota(jnp.int32, (mid, mid), 0) >= lax.broadcasted_iota(
                    jnp.int32, (mid, mid), 1
                )
                value = jnp.where(lower, real, imag)
            else:
                value = real if bi > bj else imag
            out_ref[0, rows, cols] = value * weight


def correlate_call(odd, spectra, scale_row, scale_col, visibilities, first, count, groups, channels):
    total = scale_row.shape[1]
    block = CORRELATE_BLOCK

    def place(q, slot, odd):
        at = first + q * block + slot
        return (jnp.where(odd[0] == 1, (SLOTS - at) % SLOTS, at), 0, 0)

    operands = [odd, spectra, scale_row, scale_col]
    in_specs = [
        pl.BlockSpec((spectra.shape[0], 2 * block, 8, LANES), lambda q, slot, odd: (0, q, 0, 0)),
        pl.BlockSpec((1, total), lambda q, slot, odd: (0, 0)),
        pl.BlockSpec((total, 1), lambda q, slot, odd: (0, 0)),
    ]
    aliases = {}
    if visibilities is not None:
        operands.append(visibilities)
        in_specs.append(pl.BlockSpec(memory_space=pl.ANY))
        aliases = {4: 0}
    depth = 2 * spectra.shape[0] // groups * 16
    return pl.pallas_call(
        functools.partial(correlate_body, groups),
        name="correlate",
        grid_spec=pltpu.PrefetchScalarGridSpec(
            num_scalar_prefetch=1,
            grid=(count // block, block),
            in_specs=in_specs,
            out_specs=pl.BlockSpec((1, total, total), place),
            scratch_shapes=[
                pltpu.VMEM((total, depth), jnp.bfloat16),
                pltpu.VMEM((total, depth), jnp.bfloat16),
            ],
        ),
        out_shape=jax.ShapeDtypeStruct((channels, total, total), jnp.float32),
        input_output_aliases=aliases,
        compiler_params=pltpu.CompilerParams(vmem_limit_bytes=56 * 2**20),
    )(*operands)


def trig_tables():
    dest = np.arange(LANES)[:, None]
    sample = np.arange(LANES)[None, :]
    angle = 2 * np.pi / 256 * ((dest * sample) % 256)
    offset = np.stack([np.arange(SLOTS), (SLOTS - np.arange(SLOTS)) % SLOTS], axis=1)
    twist = 2 * np.pi / 4096 * (offset[:, :, None] * np.arange(LANES)[None, None, :])
    tables = (np.cos(angle), np.sin(angle), np.cos(twist), np.sin(twist))
    return [jnp.asarray(table, jnp.float32) for table in tables]


def gains_body(gain_ref, out_ref, turned_ref):
    inputs, channels = gain_ref.shape
    half = LANES // 2
    for block in range(channels // LANES):
        piece = gain_ref[:, block * LANES : (block + 1) * LANES]
        doubled = jnp.concatenate([piece] * (LANES // inputs), axis=0)
        turned_ref[block * LANES : (block + 1) * LANES, :] = doubled.T
    for q in range(SLOTS):
        out_ref[q, pl.ds(0, half, stride=2), :] = turned_ref[pl.ds(q, half, stride=2 * SLOTS), :]
        mirror = SLOTS + (SLOTS - q) % SLOTS
        out_ref[q, pl.ds(1, half, stride=2), :] = turned_ref[
            pl.ds(mirror, half, stride=2 * SLOTS), :
        ]


def arrange_gains(gains):
    inputs, channels = gains.shape
    return pl.pallas_call(
        gains_body,
        name="gains",
        out_shape=jax.ShapeDtypeStruct((SLOTS, channels // SLOTS, LANES), jnp.float32),
        scratch_shapes=[pltpu.VMEM((channels, LANES), jnp.float32)],
    )(gains)


def per_device(voltages, pfb_taps, eq_gains):
    inputs, frames, length = voltages.shape
    stations, times = lax.axis_size("stn"), lax.axis_size("tm")
    channels = eq_gains.shape[1]
    here = lax.axis_index("tm")
    forward = [(i, i + 1) for i in range(times - 1)]
    backward = [((i + 1) % times, i) for i in range(times)]
    flag = jnp.where(here == times - 1, 0.0, 1.0).astype(jnp.float32).reshape(1)
    halos, start, source = [], 0, voltages
    for index, size in enumerate(INPUT_CHUNKS):
        block = source[start : start + size]
        ends = (block[:, frames - HALO :], block[:, :HALO])
        start += size
        if index == 0:
            source, *ends = lax.optimization_barrier((source, *ends))
        if index >= IN_FLIGHT:
            ends = lax.optimization_barrier((*ends, *halos[index - IN_FLIGHT]))[:2]
        halos.append(
            (lax.ppermute(ends[0], "tm", forward), lax.ppermute(ends[1], "tm", backward))
        )
    gains = arrange_gains(eq_gains)
    tables = trig_tables()
    partial, start = None, 0
    for size, (before, after) in zip(INPUT_CHUNKS, halos):
        partial = filter_call(flag, voltages, before, after, pfb_taps, partial, start)
        start += size
    payloads, powers, first = [], [], 0
    for index, count in enumerate(Q_CHUNKS):
        spare = 1 if index == POWER_CHUNK else 0
        payload, power = spectrum_call(partial, tables, gains, first, count, spare)
        payloads.append(payload)
        powers.append(power)
        first += count
    payloads[POWER_CHUNK] = stamp_call(powers, payloads[POWER_CHUNK])
    received = [
        lax.all_to_all(payload, ("stn", "tm"), split_axis=0, concat_axis=0, tiled=True)
        for payload in payloads
    ]
    parts = received[POWER_CHUNK][:, 2 * Q_CHUNKS[POWER_CHUNK], :3].astype(jnp.float32)
    parts = parts.reshape(stations, times, 3, LANES // inputs, inputs)
    power = jnp.sum(parts, axis=(1, 2, 3)).reshape(stations * inputs)
    all_frames = frames * times
    scale = lax.rsqrt(power / (all_frames * channels) + 1e-06)
    scale_row = (scale / all_frames).reshape(1, -1)
    scale_col = scale.reshape(-1, 1)
    odd = (here % 2).astype(jnp.int32).reshape(1)
    visibilities, first = None, 0
    for index, count in enumerate(Q_CHUNKS):
        visibilities = correlate_call(
            odd,
            received[index],
            scale_row,
            scale_col,
            visibilities,
            first,
            count,
            stations,
            channels // (stations * times),
        )
        first += count
    return visibilities


def solution(mesh):
    in_specs = (P("stn", "tm", None), P(), P("stn", None))
    out_specs = P(("stn", "tm"), None, None)
    return jax.shard_map(
        per_device, mesh=mesh, in_specs=in_specs, out_specs=out_specs, check_vma=False
    )
```

```python
import functools
import math

import jax
import jax.numpy as jnp
import numpy as np
from jax import lax
from jax.experimental import pallas as pl
from jax.experimental.pallas import tpu as pltpu
from jax.sharding import PartitionSpec as P

LANES = 128
RADIX = 32
SLOTS = 16
TAPS = 16
HALO = 8
PITCH = 40
GROUP = 8
Q_CHUNKS = (13, 3)
IN_FLIGHT = 3
SPECTRUM_BLOCK = 4
CORRELATE_BLOCK = 1
INPUT_CHUNKS = (24, 24, 16)


def real_dft(values):
    count = len(values)
    if count == 1:
        return [(values[0], None)]
    if count == 2:
        return [(values[0] + values[1], None), (values[0] - values[1], None)]
    even = real_dft(values[0::2])
    odd = real_dft(values[1::2])
    half, quarter = count // 2, count // 4
    bins = [None] * (half + 1)
    bins[0] = (even[0][0] + odd[0][0], None)
    bins[half] = (even[0][0] - odd[0][0], None)
    bins[quarter] = (even[quarter][0], -odd[quarter][0])
    for k in range(1, quarter):
        c, s = math.cos(2 * math.pi * k / count), math.sin(2 * math.pi * k / count)
        re, im = odd[k]
        if 8 * k == count:
            turned_re, turned_im = (re + im) * c, (im - re) * c
        else:
            turned_re, turned_im = re * c + im * s, im * c - re * s
        bins[k] = (even[k][0] + turned_re, even[k][1] + turned_im)
        bins[half - k] = (even[k][0] - turned_re, turned_im - even[k][1])
    return bins


def filter_body(flag_ref, own_ref, before_ref, after_ref, taps_ref, *rest):
    out_ref, frames_ref, filtered_ref = rest[-3:]
    tiles = own_ref.shape[2] // LANES
    frames = own_ref.shape[1]
    span = GROUP * PITCH
    flag = flag_ref[0]

    def widen(tile, carry):
        lanes = pl.ds(pl.multiple_of(tile * LANES, LANES), LANES)
        own = own_ref[:, :, lanes].astype(jnp.float32)
        before = before_ref[:, :, lanes].astype(jnp.float32)
        after = after_ref[:, :, lanes].astype(jnp.float32)
        for i in range(GROUP):
            row = pl.multiple_of(tile * span + i * PITCH, 8)
            frames_ref[pl.ds(row, HALO), :] = before[i]
            frames_ref[pl.ds(row + HALO, frames), :] = own[i]
            frames_ref[pl.ds(row + HALO + frames, HALO), :] = after[i]
        return carry

    lax.fori_loop(0, tiles, widen, 0)

    def fir(tile, carry):
        lanes = pl.ds(pl.multiple_of(tile * LANES, LANES), LANES)
        taps = [
            jnp.broadcast_to(taps_ref[p : p + 1, lanes], (GROUP, LANES)) for p in range(TAPS)
        ]
        even_taps, odd_taps = taps[0::2], taps[1::2]
        both_taps = [a + b for a, b in zip(even_taps, odd_taps)]
        depth = TAPS // 2

        def frame(row, half):
            value = frames_ref[pl.ds(tile * span + row, GROUP, stride=PITCH), :]
            return value * flag if half == 1 and row < HALO + frames else value

        def add(sums, at, term):
            sums[at] = sums[at] + term if at in sums else term

        for half in range(2):
            base = 4 * half
            evens, odds, boths = {}, {}, {}
            for s in range(base, base + 12):
                odd = frame(2 * s + 1, half)
                for i in range(base - 1, base + 4):
                    if 0 <= i + depth - s < depth:
                        add(odds, i, odd_taps[i + depth - s] * odd)
                if s == base:
                    continue
                even = frame(2 * s, half)
                both = even + odd
                for i in range(base, base + 4):
                    if 0 <= i + depth - s < depth:
                        add(evens, i, even_taps[i + depth - s] * even)
                        add(boths, i, both_taps[i + depth - s] * both)
            for i in range(base, base + 4):
                filtered_ref[2 * i, tile] = evens[i] + odds[i - 1]
                filtered_ref[2 * i + 1, tile] = boths[i] - evens[i] - odds[i]
        return carry

    lax.fori_loop(0, tiles, fir, 0)

    def butterfly(frame, carry):
        bins = real_dft([filtered_ref[frame, tile] for tile in range(tiles)])
        out_ref[0, frame, :, :LANES] = bins[0][0]
        out_ref[0, frame, :, LANES:] = bins[RADIX // 2][0]
        for q in range(1, SLOTS):
            out_ref[q, frame, :, :LANES] = bins[q][0]
            out_ref[q, frame, :, LANES:] = bins[q][1]
        return carry

    lax.fori_loop(0, frames, butterfly, 0)


def filter_call(flag, voltages, before, after, taps, partial, start):
    inputs, frames, length = voltages.shape
    groups = before.shape[0] // GROUP
    base = start // GROUP
    tiles = length // LANES
    operands = [flag, voltages, before, after, taps]
    in_specs = [
        pl.BlockSpec(memory_space=pltpu.SMEM),
        pl.BlockSpec((GROUP, frames, length), lambda g: (g + base, 0, 0)),
        pl.BlockSpec((GROUP, HALO, length), lambda g: (g, 0, 0)),
        pl.BlockSpec((GROUP, HALO, length), lambda g: (g, 0, 0)),
        pl.BlockSpec((TAPS, length), lambda g: (0, 0)),
    ]
    aliases = {}
    if partial is not None:
        operands.append(partial)
        in_specs.append(pl.BlockSpec(memory_space=pl.ANY))
        aliases = {5: 0}
    return pl.pallas_call(
        filter_body,
        name="filter",
        cost_estimate=pl.CostEstimate(
            flops=groups * 5 * 10**9, transcendentals=0, bytes_accessed=groups * 4 * 2**20
        ),
        grid=(groups,),
        in_specs=in_specs,
        out_specs=pl.BlockSpec((SLOTS, frames, GROUP, 2 * LANES), lambda g: (0, 0, g + base, 0)),
        out_shape=jax.ShapeDtypeStruct((SLOTS, frames, inputs, 2 * LANES), jnp.float32),
        scratch_shapes=[
            pltpu.VMEM((tiles * GROUP * PITCH, LANES), jnp.float32),
            pltpu.VMEM((frames, tiles, GROUP, LANES), jnp.float32),
        ],
        input_output_aliases=aliases,
        compiler_params=pltpu.CompilerParams(vmem_limit_bytes=56 * 2**20),
    )(*operands)


def matmul_nt(left, right):
    return lax.dot_general(
        left, right, (((1,), (1,)), ((), ())), preferred_element_type=jnp.float32
    )


def split(value):
    high = value.astype(jnp.bfloat16)
    return high, (value - high.astype(jnp.float32)).astype(jnp.bfloat16)


def spectrum_body(
    part_ref,
    cos_ref,
    sin_ref,
    twist_cos_ref,
    twist_sin_ref,
    gain_ref,
    early_ref,
    late_ref,
    power_ref,
    turn_ref,
):
    step = pl.program_id(0)
    slots, frames, inputs, width = part_ref.shape
    rows = frames * inputs
    odd = lax.broadcasted_iota(jnp.int32, (LANES, LANES), 0) % 2 == 1
    flip = jnp.where(odd, -1.0, 1.0)
    per_block = width // LANES
    total = None
    for slot in range(slots):
        twist_cos = jnp.where(odd, twist_cos_ref[slot, 1:2, :], twist_cos_ref[slot, 0:1, :])
        twist_sin = jnp.where(odd, twist_sin_ref[slot, 1:2, :], twist_sin_ref[slot, 0:1, :])
        cos = cos_ref[...] * twist_cos - sin_ref[...] * twist_sin
        sin = sin_ref[...] * twist_cos + cos_ref[...] * twist_sin
        parts = [cos, flip * sin, -sin, flip * cos]
        if slot == 0:
            special = jnp.where(step == 0, 1.0, 0.0)
            drop = jnp.where(odd, special, 0.0)
            keep = 1.0 - drop
            sign = flip * (1.0 - special)
            parts = [cos * keep, sign * sin + drop * cos, -sin * keep, sign * cos - drop * sin]
        matrix = jnp.concatenate(
            [jnp.concatenate(parts[:2], axis=1), jnp.concatenate(parts[2:], axis=1)], axis=0
        )
        matrix_high, matrix_low = split(matrix)
        part = part_ref[slot].reshape(rows, width)
        gain = gain_ref[slot]
        for block in range(rows // width):
            part_high, part_low = split(part[block * width : (block + 1) * width])
            spec = (
                matmul_nt(matrix_high, part_high)
                + matmul_nt(matrix_high, part_low)
                + matmul_nt(matrix_low, part_high)
            )
            for side in range(2):
                for tile in range(per_block):
                    value = spec[
                        side * LANES : (side + 1) * LANES, tile * LANES : (tile + 1) * LANES
                    ]
                    turn_ref[slot % 2, side, pl.ds(block * per_block + tile, LANES, stride=8), :] = (
                        value * gain
                    )
        for side in range(2):
            rounded = turn_ref[slot % 2, side].reshape(LANES, 8, LANES).astype(jnp.bfloat16)
            early_ref[:, 2 * slot + side] = rounded
            if slot >= slots - Q_CHUNKS[1]:
                late_ref[:, 2 * (slot - slots + Q_CHUNKS[1]) + side] = rounded
            wide = rounded.astype(jnp.float32)
            power = jnp.sum(wide * wide, axis=0)
            total = power if total is None else total + power

    @pl.when(step == 0)
    def _():
        power_ref[...] = total

    @pl.when(step > 0)
    def _():
        power_ref[...] += total

    @pl.when(step == pl.num_programs(0) - 1)
    def _():
        power = jnp.sum(power_ref[...], axis=0, keepdims=True)
        high = power.astype(jnp.bfloat16).astype(jnp.float32)
        middle = (power - high).astype(jnp.bfloat16).astype(jnp.float32)
        low = power - high - middle
        row = lax.broadcasted_iota(jnp.int32, (8, LANES), 0)
        tile = jnp.where(row == 0, high, jnp.where(row == 1, middle, jnp.where(row == 2, low, 0.0)))
        early_ref[:, 2 * (slots - Q_CHUNKS[1])] = jnp.broadcast_to(
            tile.astype(jnp.bfloat16)[None], (LANES, 8, LANES)
        )


def spectrum_call(partial, tables, gains):
    _, frames, inputs, width = partial.shape
    block = SPECTRUM_BLOCK
    whole = lambda q: (0, 0)
    pick = lambda q: (q, 0, 0)
    early, late = Q_CHUNKS
    return pl.pallas_call(
        spectrum_body,
        name="spectrum",
        grid=(SLOTS // block,),
        in_specs=[
            pl.BlockSpec((block, frames, inputs, width), lambda q: (q, 0, 0, 0)),
            pl.BlockSpec((LANES, LANES), whole),
            pl.BlockSpec((LANES, LANES), whole),
            pl.BlockSpec((block, 2, LANES), pick),
            pl.BlockSpec((block, 2, LANES), pick),
            pl.BlockSpec((block, LANES, LANES), pick),
        ],
        out_specs=[
            pl.BlockSpec((LANES, 2 * block, 8, LANES), lambda q: (0, q, 0, 0)),
            pl.BlockSpec((LANES, 2 * late, 8, LANES), lambda q: (0, 0, 0, 0)),
        ],
        out_shape=[
            jax.ShapeDtypeStruct((LANES, 2 * early + 1, 8, LANES), jnp.bfloat16),
            jax.ShapeDtypeStruct((LANES, 2 * late, 8, LANES), jnp.bfloat16),
        ],
        scratch_shapes=[
            pltpu.VMEM((8, LANES), jnp.float32),
            pltpu.VMEM((2, 2, 8 * LANES, LANES), jnp.float32),
        ],
        compiler_params=pltpu.CompilerParams(vmem_limit_bytes=56 * 2**20),
    )(partial, *tables, gains)


def correlate_body(groups, odd_ref, spec_ref, row_ref, col_ref, *rest):
    out_ref, left_ref, swapped_ref = rest[-3:]
    slot = pl.program_id(1)
    blocks = spec_ref.shape[0] // groups
    half = LANES // 2
    depth = blocks * 8
    for side in range(2):
        for s in range(groups):
            tile = spec_ref[s * blocks : (s + 1) * blocks, 2 * slot + side].reshape(depth, LANES).T
            rows = slice(s * half, (s + 1) * half)
            for part in range(2):
                piece = tile[part * half : (part + 1) * half]
                at = part * depth
                left_ref[rows, side * 2 * depth + at : side * 2 * depth + at + depth] = piece
                other = (1 - side) * 2 * depth + at
                swapped_ref[rows, other : other + depth] = -piece if side == 0 else piece
    total = groups * half
    mid = total // 2
    for bi in range(2):
        for bj in range(2):
            rows, cols = slice(bi * mid, (bi + 1) * mid), slice(bj * mid, (bj + 1) * mid)
            weight = col_ref[rows, :] * row_ref[:, cols]
            right = left_ref[cols, :]
            if bi >= bj:
                real = matmul_nt(left_ref[rows, :], right)
            if bi <= bj:
                imag = matmul_nt(swapped_ref[rows, :], right)
            if bi == bj:
                lower = lax.broadcasted_iota(jnp.int32, (mid, mid), 0) >= lax.broadcasted_iota(
                    jnp.int32, (mid, mid), 1
                )
                value = jnp.where(lower, real, imag)
            else:
                value = real if bi > bj else imag
            out_ref[0, rows, cols] = value * weight


def correlate_call(odd, spectra, scale_row, scale_col, visibilities, first, count, groups, channels):
    total = scale_row.shape[1]
    block = CORRELATE_BLOCK

    def place(q, slot, odd):
        at = first + q * block + slot
        return (jnp.where(odd[0] == 1, (SLOTS - at) % SLOTS, at), 0, 0)

    operands = [odd, spectra, scale_row, scale_col]
    in_specs = [
        pl.BlockSpec((spectra.shape[0], 2 * block, 8, LANES), lambda q, slot, odd: (0, q, 0, 0)),
        pl.BlockSpec((1, total), lambda q, slot, odd: (0, 0)),
        pl.BlockSpec((total, 1), lambda q, slot, odd: (0, 0)),
    ]
    aliases = {}
    if visibilities is not None:
        operands.append(visibilities)
        in_specs.append(pl.BlockSpec(memory_space=pl.ANY))
        aliases = {4: 0}
    depth = 2 * spectra.shape[0] // groups * 16
    return pl.pallas_call(
        functools.partial(correlate_body, groups),
        name="correlate",
        grid_spec=pltpu.PrefetchScalarGridSpec(
            num_scalar_prefetch=1,
            grid=(count // block, block),
            in_specs=in_specs,
            out_specs=pl.BlockSpec((1, total, total), place),
            scratch_shapes=[
                pltpu.VMEM((total, depth), jnp.bfloat16),
                pltpu.VMEM((total, depth), jnp.bfloat16),
            ],
        ),
        out_shape=jax.ShapeDtypeStruct((channels, total, total), jnp.float32),
        input_output_aliases=aliases,
        compiler_params=pltpu.CompilerParams(vmem_limit_bytes=56 * 2**20),
    )(*operands)


def trig_tables():
    dest = np.arange(LANES)[:, None]
    sample = np.arange(LANES)[None, :]
    angle = 2 * np.pi / 256 * ((dest * sample) % 256)
    offset = np.stack([np.arange(SLOTS), (SLOTS - np.arange(SLOTS)) % SLOTS], axis=1)
    twist = 2 * np.pi / 4096 * (offset[:, :, None] * np.arange(LANES)[None, None, :])
    tables = (np.cos(angle), np.sin(angle), np.cos(twist), np.sin(twist))
    return [jnp.asarray(table, jnp.float32) for table in tables]


def gains_body(gain_ref, out_ref, turned_ref):
    inputs, channels = gain_ref.shape
    half = LANES // 2
    for block in range(channels // LANES):
        piece = gain_ref[:, block * LANES : (block + 1) * LANES]
        doubled = jnp.concatenate([piece] * (LANES // inputs), axis=0)
        turned_ref[block * LANES : (block + 1) * LANES, :] = doubled.T
    for q in range(SLOTS):
        out_ref[q, pl.ds(0, half, stride=2), :] = turned_ref[pl.ds(q, half, stride=2 * SLOTS), :]
        mirror = SLOTS + (SLOTS - q) % SLOTS
        out_ref[q, pl.ds(1, half, stride=2), :] = turned_ref[
            pl.ds(mirror, half, stride=2 * SLOTS), :
        ]


def arrange_gains(gains):
    inputs, channels = gains.shape
    return pl.pallas_call(
        gains_body,
        name="gains",
        out_shape=jax.ShapeDtypeStruct((SLOTS, channels // SLOTS, LANES), jnp.float32),
        scratch_shapes=[pltpu.VMEM((channels, LANES), jnp.float32)],
    )(gains)


def per_device(voltages, pfb_taps, eq_gains):
    inputs, frames, length = voltages.shape
    stations, times = lax.axis_size("stn"), lax.axis_size("tm")
    channels = eq_gains.shape[1]
    here = lax.axis_index("tm")
    forward = [(i, i + 1) for i in range(times - 1)]
    backward = [((i + 1) % times, i) for i in range(times)]
    flag = jnp.where(here == times - 1, 0.0, 1.0).astype(jnp.float32).reshape(1)
    halos, start, source = [], 0, voltages
    for index, size in enumerate(INPUT_CHUNKS):
        block = source[start : start + size]
        ends = (block[:, frames - HALO :], block[:, :HALO])
        start += size
        if index == 0:
            source, *ends = lax.optimization_barrier((source, *ends))
        if index >= IN_FLIGHT:
            ends = lax.optimization_barrier((*ends, *halos[index - IN_FLIGHT]))[:2]
        halos.append(
            (lax.ppermute(ends[0], "tm", forward), lax.ppermute(ends[1], "tm", backward))
        )
    gains = arrange_gains(eq_gains)
    tables = trig_tables()
    partial, start = None, 0
    for size, (before, after) in zip(INPUT_CHUNKS, halos):
        partial = filter_call(flag, voltages, before, after, pfb_taps, partial, start)
        start += size
    payloads = spectrum_call(partial, tables, gains)
    received = [
        lax.all_to_all(payload, ("stn", "tm"), split_axis=0, concat_axis=0, tiled=True)
        for payload in payloads
    ]
    parts = received[0][:, 2 * Q_CHUNKS[0], :3].astype(jnp.float32)
    parts = parts.reshape(stations, times, 3, LANES // inputs, inputs)
    power = jnp.sum(parts, axis=(1, 2, 3)).reshape(stations * inputs)
    all_frames = frames * times
    scale = lax.rsqrt(power / (all_frames * channels) + 1e-06)
    scale_row = (scale / all_frames).reshape(1, -1)
    scale_col = scale.reshape(-1, 1)
    odd = (here % 2).astype(jnp.int32).reshape(1)
    visibilities, first = None, 0
    for index, count in enumerate(Q_CHUNKS):
        visibilities = correlate_call(
            odd,
            received[index],
            scale_row,
            scale_col,
            visibilities,
            first,
            count,
            stations,
            channels // (stations * times),
        )
        first += count
    return visibilities


def solution(mesh):
    in_specs = (P("stn", "tm", None), P(), P("stn", None))
    out_specs = P(("stn", "tm"), None, None)
    return jax.shard_map(
        per_device, mesh=mesh, in_specs=in_specs, out_specs=out_specs, check_vma=False
    )
```

```python
import functools
import math

import jax
import jax.numpy as jnp
import numpy as np
from jax import lax
from jax.experimental import pallas as pl
from jax.experimental.pallas import tpu as pltpu
from jax.sharding import PartitionSpec as P

LANES = 128
RADIX = 32
SLOTS = 16
TAPS = 16
HALO = 8
PITCH = 40
GROUP = 8
Q_CHUNKS = (13, 3)
IN_FLIGHT = 3
SPECTRUM_BLOCK = 4
CORRELATE_BLOCK = 1
INPUT_CHUNKS = (24, 24, 16)


def real_dft(values):
    count = len(values)
    if count == 1:
        return [(values[0], None)]
    if count == 2:
        return [(values[0] + values[1], None), (values[0] - values[1], None)]
    even = real_dft(values[0::2])
    odd = real_dft(values[1::2])
    half, quarter = count // 2, count // 4
    bins = [None] * (half + 1)
    bins[0] = (even[0][0] + odd[0][0], None)
    bins[half] = (even[0][0] - odd[0][0], None)
    bins[quarter] = (even[quarter][0], -odd[quarter][0])
    for k in range(1, quarter):
        c, s = math.cos(2 * math.pi * k / count), math.sin(2 * math.pi * k / count)
        re, im = odd[k]
        if 8 * k == count:
            turned_re, turned_im = (re + im) * c, (im - re) * c
        else:
            turned_re, turned_im = re * c + im * s, im * c - re * s
        bins[k] = (even[k][0] + turned_re, even[k][1] + turned_im)
        bins[half - k] = (even[k][0] - turned_re, turned_im - even[k][1])
    return bins


def filter_body(flag_ref, own_ref, before_ref, after_ref, taps_ref, *rest):
    out_ref, frames_ref, filtered_ref = rest[-3:]
    tiles = own_ref.shape[2] // LANES
    frames = own_ref.shape[1]
    span = GROUP * PITCH
    flag = flag_ref[0]

    def widen(tile, carry):
        lanes = pl.ds(pl.multiple_of(tile * LANES, LANES), LANES)
        own = own_ref[:, :, lanes].astype(jnp.float32)
        before = before_ref[:, :, lanes].astype(jnp.float32)
        after = after_ref[:, :, lanes].astype(jnp.float32)
        for i in range(GROUP):
            row = pl.multiple_of(tile * span + i * PITCH, 8)
            frames_ref[pl.ds(row, HALO), :] = before[i]
            frames_ref[pl.ds(row + HALO, frames), :] = own[i]
            frames_ref[pl.ds(row + HALO + frames, HALO), :] = after[i]
        return carry

    lax.fori_loop(0, tiles, widen, 0)

    def fir(tile, carry):
        lanes = pl.ds(pl.multiple_of(tile * LANES, LANES), LANES)
        taps = [
            jnp.broadcast_to(taps_ref[p : p + 1, lanes], (GROUP, LANES)) for p in range(TAPS)
        ]
        even_taps, odd_taps = taps[0::2], taps[1::2]
        both_taps = [a + b for a, b in zip(even_taps, odd_taps)]
        depth = TAPS // 2

        def frame(row, half):
            value = frames_ref[pl.ds(tile * span + row, GROUP, stride=PITCH), :]
            return value * flag if half == 1 and row < HALO + frames else value

        def add(sums, at, term):
            sums[at] = sums[at] + term if at in sums else term

        for half in range(2):
            base = 4 * half
            evens, odds, boths = {}, {}, {}
            for s in range(base, base + 12):
                odd = frame(2 * s + 1, half)
                for i in range(base - 1, base + 4):
                    if 0 <= i + depth - s < depth:
                        add(odds, i, odd_taps[i + depth - s] * odd)
                if s == base:
                    continue
                even = frame(2 * s, half)
                both = even + odd
                for i in range(base, base + 4):
                    if 0 <= i + depth - s < depth:
                        add(evens, i, even_taps[i + depth - s] * even)
                        add(boths, i, both_taps[i + depth - s] * both)
            for i in range(base, base + 4):
                filtered_ref[2 * i, tile] = evens[i] + odds[i - 1]
                filtered_ref[2 * i + 1, tile] = boths[i] - evens[i] - odds[i]
        return carry

    lax.fori_loop(0, tiles, fir, 0)

    def butterfly(frame, carry):
        bins = real_dft([filtered_ref[frame, tile] for tile in range(tiles)])
        out_ref[0, frame, :, :LANES] = bins[0][0]
        out_ref[0, frame, :, LANES:] = bins[RADIX // 2][0]
        for q in range(1, SLOTS):
            out_ref[q, frame, :, :LANES] = bins[q][0]
            out_ref[q, frame, :, LANES:] = bins[q][1]
        return carry

    lax.fori_loop(0, frames, butterfly, 0)


def filter_call(flag, voltages, before, after, taps, partial, start):
    inputs, frames, length = voltages.shape
    groups = before.shape[0] // GROUP
    base = start // GROUP
    tiles = length // LANES
    operands = [flag, voltages, before, after, taps]
    in_specs = [
        pl.BlockSpec(memory_space=pltpu.SMEM),
        pl.BlockSpec((GROUP, frames, length), lambda g: (g + base, 0, 0)),
        pl.BlockSpec((GROUP, HALO, length), lambda g: (g, 0, 0)),
        pl.BlockSpec((GROUP, HALO, length), lambda g: (g, 0, 0)),
        pl.BlockSpec((TAPS, length), lambda g: (0, 0)),
    ]
    aliases = {}
    if partial is not None:
        operands.append(partial)
        in_specs.append(pl.BlockSpec(memory_space=pl.ANY))
        aliases = {5: 0}
    return pl.pallas_call(
        filter_body,
        name="filter",
        cost_estimate=pl.CostEstimate(
            flops=groups * 5 * 10**9, transcendentals=0, bytes_accessed=groups * 4 * 2**20
        ),
        grid=(groups,),
        in_specs=in_specs,
        out_specs=pl.BlockSpec((SLOTS, frames, GROUP, 2 * LANES), lambda g: (0, 0, g + base, 0)),
        out_shape=jax.ShapeDtypeStruct((SLOTS, frames, inputs, 2 * LANES), jnp.float32),
        scratch_shapes=[
            pltpu.VMEM((tiles * GROUP * PITCH, LANES), jnp.float32),
            pltpu.VMEM((frames, tiles, GROUP, LANES), jnp.float32),
        ],
        input_output_aliases=aliases,
        compiler_params=pltpu.CompilerParams(vmem_limit_bytes=49 * 2**20),
    )(*operands)


def matmul_nt(left, right):
    return lax.dot_general(
        left, right, (((1,), (1,)), ((), ())), preferred_element_type=jnp.float32
    )


def split(value):
    high = value.astype(jnp.bfloat16)
    return high, (value - high.astype(jnp.float32)).astype(jnp.bfloat16)


def spectrum_body(
    part_ref,
    cos_ref,
    sin_ref,
    twist_cos_ref,
    twist_sin_ref,
    gain_ref,
    early_ref,
    late_ref,
    power_ref,
    turn_ref,
):
    step = pl.program_id(0)
    slots, frames, inputs, width = part_ref.shape
    rows = frames * inputs
    odd = lax.broadcasted_iota(jnp.int32, (LANES, LANES), 0) % 2 == 1
    flip = jnp.where(odd, -1.0, 1.0)
    per_block = width // LANES
    total = None
    for slot in range(slots):
        twist_cos = jnp.where(odd, twist_cos_ref[slot, 1:2, :], twist_cos_ref[slot, 0:1, :])
        twist_sin = jnp.where(odd, twist_sin_ref[slot, 1:2, :], twist_sin_ref[slot, 0:1, :])
        cos = cos_ref[...] * twist_cos - sin_ref[...] * twist_sin
        sin = sin_ref[...] * twist_cos + cos_ref[...] * twist_sin
        parts = [cos, flip * sin, -sin, flip * cos]
        if slot == 0:
            special = jnp.where(step == 0, 1.0, 0.0)
            drop = jnp.where(odd, special, 0.0)
            keep = 1.0 - drop
            sign = flip * (1.0 - special)
            parts = [cos * keep, sign * sin + drop * cos, -sin * keep, sign * cos - drop * sin]
        matrix = jnp.concatenate(
            [jnp.concatenate(parts[:2], axis=1), jnp.concatenate(parts[2:], axis=1)], axis=0
        )
        matrix_high, matrix_low = split(matrix)
        part = part_ref[slot].reshape(rows, width)
        gain = gain_ref[slot]
        for block in range(rows // width):
            part_high, part_low = split(part[block * width : (block + 1) * width])
            spec = (
                matmul_nt(matrix_high, part_high)
                + matmul_nt(matrix_high, part_low)
                + matmul_nt(matrix_low, part_high)
            )
            for side in range(2):
                for tile in range(per_block):
                    value = spec[
                        side * LANES : (side + 1) * LANES, tile * LANES : (tile + 1) * LANES
                    ]
                    turn_ref[slot % 2, side, pl.ds(block * per_block + tile, LANES, stride=8), :] = (
                        value * gain
                    )
        for side in range(2):
            rounded = turn_ref[slot % 2, side].reshape(LANES, 8, LANES).astype(jnp.bfloat16)
            early_ref[:, 2 * slot + side] = rounded
            if slot >= slots - Q_CHUNKS[1]:
                late_ref[:, 2 * (slot - slots + Q_CHUNKS[1]) + side] = rounded
            wide = rounded.astype(jnp.float32)
            power = jnp.sum(wide * wide, axis=0)
            total = power if total is None else total + power

    @pl.when(step == 0)
    def _():
        power_ref[...] = total

    @pl.when(step > 0)
    def _():
        power_ref[...] += total

    @pl.when(step == pl.num_programs(0) - 1)
    def _():
        power = jnp.sum(power_ref[...], axis=0, keepdims=True)
        high = power.astype(jnp.bfloat16).astype(jnp.float32)
        middle = (power - high).astype(jnp.bfloat16).astype(jnp.float32)
        low = power - high - middle
        row = lax.broadcasted_iota(jnp.int32, (8, LANES), 0)
        tile = jnp.where(row == 0, high, jnp.where(row == 1, middle, jnp.where(row == 2, low, 0.0)))
        early_ref[:, 2 * (slots - Q_CHUNKS[1])] = jnp.broadcast_to(
            tile.astype(jnp.bfloat16)[None], (LANES, 8, LANES)
        )


def spectrum_call(partial, tables, gains):
    _, frames, inputs, width = partial.shape
    block = SPECTRUM_BLOCK
    whole = lambda q: (0, 0)
    pick = lambda q: (q, 0, 0)
    early, late = Q_CHUNKS
    return pl.pallas_call(
        spectrum_body,
        name="spectrum",
        grid=(SLOTS // block,),
        in_specs=[
            pl.BlockSpec((block, frames, inputs, width), lambda q: (q, 0, 0, 0)),
            pl.BlockSpec((LANES, LANES), whole),
            pl.BlockSpec((LANES, LANES), whole),
            pl.BlockSpec((block, 2, LANES), pick),
            pl.BlockSpec((block, 2, LANES), pick),
            pl.BlockSpec((block, LANES, LANES), pick),
        ],
        out_specs=[
            pl.BlockSpec((LANES, 2 * block, 8, LANES), lambda q: (0, q, 0, 0)),
            pl.BlockSpec((LANES, 2 * late, 8, LANES), lambda q: (0, 0, 0, 0)),
        ],
        out_shape=[
            jax.ShapeDtypeStruct((LANES, 2 * early + 1, 8, LANES), jnp.bfloat16),
            jax.ShapeDtypeStruct((LANES, 2 * late, 8, LANES), jnp.bfloat16),
        ],
        scratch_shapes=[
            pltpu.VMEM((8, LANES), jnp.float32),
            pltpu.VMEM((2, 2, 8 * LANES, LANES), jnp.float32),
        ],
        compiler_params=pltpu.CompilerParams(vmem_limit_bytes=56 * 2**20),
    )(partial, *tables, gains)


def correlate_body(groups, odd_ref, spec_ref, row_ref, col_ref, *rest):
    out_ref, left_ref, swapped_ref = rest[-3:]
    slot = pl.program_id(1)
    blocks = spec_ref.shape[0] // groups
    half = LANES // 2
    depth = blocks * 8
    for side in range(2):
        for s in range(groups):
            tile = spec_ref[s * blocks : (s + 1) * blocks, 2 * slot + side].reshape(depth, LANES).T
            rows = slice(s * half, (s + 1) * half)
            for part in range(2):
                piece = tile[part * half : (part + 1) * half]
                at = part * depth
                left_ref[rows, side * 2 * depth + at : side * 2 * depth + at + depth] = piece
                other = (1 - side) * 2 * depth + at
                swapped_ref[rows, other : other + depth] = -piece if side == 0 else piece
    total = groups * half
    mid = total // 2
    for bi in range(2):
        for bj in range(2):
            rows, cols = slice(bi * mid, (bi + 1) * mid), slice(bj * mid, (bj + 1) * mid)
            weight = col_ref[rows, :] * row_ref[:, cols]
            right = left_ref[cols, :]
            if bi >= bj:
                real = matmul_nt(left_ref[rows, :], right)
            if bi <= bj:
                imag = matmul_nt(swapped_ref[rows, :], right)
            if bi == bj:
                lower = lax.broadcasted_iota(jnp.int32, (mid, mid), 0) >= lax.broadcasted_iota(
                    jnp.int32, (mid, mid), 1
                )
                value = jnp.where(lower, real, imag)
            else:
                value = real if bi > bj else imag
            out_ref[0, rows, cols] = value * weight


def correlate_call(odd, spectra, scale_row, scale_col, visibilities, first, count, groups, channels):
    total = scale_row.shape[1]
    block = CORRELATE_BLOCK

    def place(q, slot, odd):
        at = first + q * block + slot
        return (jnp.where(odd[0] == 1, (SLOTS - at) % SLOTS, at), 0, 0)

    operands = [odd, spectra, scale_row, scale_col]
    in_specs = [
        pl.BlockSpec((spectra.shape[0], 2 * block, 8, LANES), lambda q, slot, odd: (0, q, 0, 0)),
        pl.BlockSpec((1, total), lambda q, slot, odd: (0, 0)),
        pl.BlockSpec((total, 1), lambda q, slot, odd: (0, 0)),
    ]
    aliases = {}
    if visibilities is not None:
        operands.append(visibilities)
        in_specs.append(pl.BlockSpec(memory_space=pl.ANY))
        aliases = {4: 0}
    depth = 2 * spectra.shape[0] // groups * 16
    return pl.pallas_call(
        functools.partial(correlate_body, groups),
        name="correlate",
        grid_spec=pltpu.PrefetchScalarGridSpec(
            num_scalar_prefetch=1,
            grid=(count // block, block),
            in_specs=in_specs,
            out_specs=pl.BlockSpec((1, total, total), place),
            scratch_shapes=[
                pltpu.VMEM((total, depth), jnp.bfloat16),
                pltpu.VMEM((total, depth), jnp.bfloat16),
            ],
        ),
        out_shape=jax.ShapeDtypeStruct((channels, total, total), jnp.float32),
        input_output_aliases=aliases,
        compiler_params=pltpu.CompilerParams(vmem_limit_bytes=20 * 2**20),
    )(*operands)


def trig_tables():
    dest = np.arange(LANES)[:, None]
    sample = np.arange(LANES)[None, :]
    angle = 2 * np.pi / 256 * ((dest * sample) % 256)
    offset = np.stack([np.arange(SLOTS), (SLOTS - np.arange(SLOTS)) % SLOTS], axis=1)
    twist = 2 * np.pi / 4096 * (offset[:, :, None] * np.arange(LANES)[None, None, :])
    tables = (np.cos(angle), np.sin(angle), np.cos(twist), np.sin(twist))
    return [jnp.asarray(table, jnp.float32) for table in tables]


def gains_body(gain_ref, out_ref, turned_ref):
    inputs, channels = gain_ref.shape
    half = LANES // 2
    for block in range(channels // LANES):
        piece = gain_ref[:, block * LANES : (block + 1) * LANES]
        doubled = jnp.concatenate([piece] * (LANES // inputs), axis=0)
        turned_ref[block * LANES : (block + 1) * LANES, :] = doubled.T
    for q in range(SLOTS):
        out_ref[q, pl.ds(0, half, stride=2), :] = turned_ref[pl.ds(q, half, stride=2 * SLOTS), :]
        mirror = SLOTS + (SLOTS - q) % SLOTS
        out_ref[q, pl.ds(1, half, stride=2), :] = turned_ref[
            pl.ds(mirror, half, stride=2 * SLOTS), :
        ]


def arrange_gains(gains):
    inputs, channels = gains.shape
    return pl.pallas_call(
        gains_body,
        name="gains",
        out_shape=jax.ShapeDtypeStruct((SLOTS, channels // SLOTS, LANES), jnp.float32),
        scratch_shapes=[pltpu.VMEM((channels, LANES), jnp.float32)],
    )(gains)


def per_device(voltages, pfb_taps, eq_gains):
    inputs, frames, length = voltages.shape
    stations, times = lax.axis_size("stn"), lax.axis_size("tm")
    channels = eq_gains.shape[1]
    here = lax.axis_index("tm")
    forward = [(i, i + 1) for i in range(times - 1)]
    backward = [((i + 1) % times, i) for i in range(times)]
    flag = jnp.where(here == times - 1, 0.0, 1.0).astype(jnp.float32).reshape(1)
    halos, start, source = [], 0, voltages
    for index, size in enumerate(INPUT_CHUNKS):
        block = source[start : start + size]
        ends = (block[:, frames - HALO :], block[:, :HALO])
        start += size
        if index == 0:
            source, *ends = lax.optimization_barrier((source, *ends))
        if index >= IN_FLIGHT:
            ends = lax.optimization_barrier((*ends, *halos[index - IN_FLIGHT]))[:2]
        halos.append(
            (lax.ppermute(ends[0], "tm", forward), lax.ppermute(ends[1], "tm", backward))
        )
    gains = arrange_gains(eq_gains)
    tables = trig_tables()
    partial, start = None, 0
    for size, (before, after) in zip(INPUT_CHUNKS, halos):
        partial = filter_call(flag, voltages, before, after, pfb_taps, partial, start)
        start += size
    payloads = spectrum_call(partial, tables, gains)
    received = [
        lax.all_to_all(payload, ("stn", "tm"), split_axis=0, concat_axis=0, tiled=True)
        for payload in payloads
    ]
    parts = received[0][:, 2 * Q_CHUNKS[0], :3].astype(jnp.float32)
    parts = parts.reshape(stations, times, 3, LANES // inputs, inputs)
    power = jnp.sum(parts, axis=(1, 2, 3)).reshape(stations * inputs)
    all_frames = frames * times
    scale = lax.rsqrt(power / (all_frames * channels) + 1e-06)
    scale_row = (scale / all_frames).reshape(1, -1)
    scale_col = scale.reshape(-1, 1)
    odd = (here % 2).astype(jnp.int32).reshape(1)
    visibilities, first = None, 0
    for index, count in enumerate(Q_CHUNKS):
        visibilities = correlate_call(
            odd,
            received[index],
            scale_row,
            scale_col,
            visibilities,
            first,
            count,
            stations,
            channels // (stations * times),
        )
        first += count
    return visibilities


def solution(mesh):
    in_specs = (P("stn", "tm", None), P(), P("stn", None))
    out_specs = P(("stn", "tm"), None, None)
    return jax.shard_map(
        per_device, mesh=mesh, in_specs=in_specs, out_specs=out_specs, check_vma=False
    )
```
